512 devices in a mesh: dp: 32 (over z, y_lo), tensor: 16 (over y_hi, x, core).
Axes of the slice: x: 4, y: 4 (y_hi: 2, y_lo: 2; y = y_hi * 2 + y_lo), z: 16, core: 2. Of those that a mesh axis runs over, the one named last changes fastest.
Arguments:
- activations: bfloat16 [32768, 8192], P('dp', 'tensor'), may hold values from -6 to 6
- out_grads: bfloat16 [32768, 8192], P('dp', 'tensor'), may hold values from -6 to 6
- proj_in: bfloat16 [8192, 64], P('tensor'), may hold values from -0.0625 to 0.0625
- proj_out: bfloat16 [8192, 64], P('tensor'), may hold values from -0.0625 to 0.0625
- segment_ids: int32 [32, 1024], P('dp'), may hold values from 0 to 23, never falling along the last dimension, each value on 1 to 80 neighbouring positions
- train_logs: bfloat16 [131072, 4096], P('dp', 'tensor'), may hold values from -6 to 6
- doc_ids: int32 [131072], P(('dp', 'tensor')), may hold values from 0 to 255
Outputs:
- scores: float32 [768, 131072], P(None, ('dp', 'tensor'))
- doc_influence: float32 [768, 256], replicated
The draws below stay inside these ranges and needn't reach their ends.
Inputs may be any that keep to these rules, and one draw needn't show every extreme that they name: `segment_ids`: in each row the example numbers never fall; each of the 24 examples has 1 to 80 tokens, and one has exactly 80.
All inputs are finite; a program needn't handle non-finite values.
Results may differ from the reference program's by a relative error of at most 0.0052.
Values may be sent and summed in bfloat16 or wider, within the bound.
No kernel may reach another device: no remote copies, remote signals or barrier semaphores. Data moves between devices by JAX's collectives and lax.ppermute only.
A program may use at most 64 MiB of HBM per device.

```python
import math
import jax
import jax.numpy as jnp
import numpy as np
from jax import lax

D = 8192
R = 64
LOG = 4096
TOK_DEV = 1024
EX_DEV = 24
MOST = 80
N_DEV = 4096
DOCS = 256
SHARDS = 32
TOKENS = 32768
N = 131072
N_DP = 32


def set_ends(entries, stream_key, smallest, high):
    index_at = [jax.random.randint(jax.random.fold_in(stream_key, axis), (), 0, length) for axis, length in enumerate(entries.shape)]
    main_axis = entries.shape.index(max(entries.shape))
    beside = index_at[:main_axis] + [(index_at[main_axis] + 1) % entries.shape[main_axis]] + index_at[main_axis + 1:]
    return entries.at[tuple(index_at)].set(smallest).at[tuple(beside)].set(high)


def shard_levels(key, dims, cuts, low, top_value):
    loudness, own = 1.0, jax.random.fold_in(key, 6)
    for position, shards_of in cuts:
        heights = jnp.exp(jax.random.uniform(jax.random.fold_in(own, position), (shards_of,), jnp.float32, low / len(cuts), top_value / len(cuts)))
        loudness = loudness * jnp.repeat(heights, dims[position] // shards_of).reshape([-1 if axis == position else 1 for axis in range(len(dims))])
    return loudness


def split_up(count, total, bound, slope):
    loads = [(1 << 20) // math.isqrt(rank ** slope) + 1 for rank in range(2, count + 1)]
    rest, holding = total - bound - (count - 1), [1] * (count - 1)
    while rest > 0:
        candidates = [i for i in range(count - 1) if holding[i] < bound]
        pool, budget = sum([loads[i] for i in candidates]), rest
        for i in candidates:
            extra = min(bound - holding[i], max(1, budget * loads[i] // pool), rest)
            holding[i] = holding[i] + extra
            rest = rest - extra
    return np.array([bound] + holding)


def ragged(rng, amount, total, reach, lean):
    if amount == 2:
        one = jax.random.randint(rng, (), max(1, total - reach), min(reach, total - 1) + 1)
        return jnp.stack([one, total - one])
    lengths = jnp.asarray(split_up(amount, total, reach, lean), jnp.int32)
    couples = (amount - 1) // 2
    source_of, receiver = lengths[1:1 + 2 * couples:2], lengths[2:2 + 2 * couples:2]
    room = jnp.minimum(source_of - 1, reach - receiver)
    passed = jax.random.randint(jax.random.fold_in(rng, 1), (couples,), 0, 1 << 20) % (room + 1)
    lengths = lengths.at[1:1 + 2 * couples:2].set(source_of - passed).at[2:2 + 2 * couples:2].set(receiver + passed)
    return lengths[jax.random.permutation(jax.random.fold_in(rng, 2), amount)]


def centred(key, dims, spread, bound, pieces=(), kind=jnp.bfloat16):
    values = spread * jax.random.normal(key, dims, jnp.float32)
    if pieces:
        values = values * shard_levels(key, dims, pieces, -0.22, 0.18)
    return jnp.clip(values, -bound, bound).astype(kind)


def setup_inputs(seed: int = 0) -> dict:
    streams_of = jax.random.split(jax.random.key(seed), 8)
    return {
        "activations": centred(streams_of[0], (TOKENS, D), 1.0, 6.0, ((0, 32), (1, 16))),
        "out_grads": centred(streams_of[1], (TOKENS, D), 1.0, 6.0, ((0, 32), (1, 16))),
        "proj_in": centred(streams_of[2], (D, R), D ** -0.5, 0.0625, ((0, 16),)),
        "proj_out": centred(streams_of[3], (D, R), D ** -0.5, 0.0625, ((0, 16),)),
        "segment_ids": jax.vmap(lambda own: jnp.searchsorted(jnp.cumsum(ragged(own, EX_DEV, TOK_DEV, MOST, 0)), jnp.arange(TOK_DEV), side="right"))(jax.random.split(streams_of[4], SHARDS)).reshape((SHARDS, TOK_DEV)).astype(jnp.int32),
        "train_logs": centred(streams_of[5], (N, LOG), 1.0, 6.0, ((0, 32), (1, 16))),
        "doc_ids": set_ends(jax.random.randint(streams_of[6], (N,), 0, DOCS), jax.random.fold_in(streams_of[6], 1), 0, DOCS - 1).astype(jnp.int32),
    }


def reference(activations, out_grads, proj_in, proj_out, segment_ids, train_logs, doc_ids):
    in_proj = jnp.dot(activations, proj_in, preferred_element_type=jnp.float32).astype(jnp.bfloat16)
    out_proj = jnp.dot(out_grads, proj_out, preferred_element_type=jnp.float32).astype(jnp.bfloat16)
    labels = jnp.arange(EX_DEV, dtype=jnp.int32)

    def one_group(group):
        rows_in = lax.dynamic_slice_in_dim(in_proj, group * TOK_DEV, TOK_DEV, 0).astype(jnp.float32)
        rows_out = lax.dynamic_slice_in_dim(out_proj, group * TOK_DEV, TOK_DEV, 0).astype(jnp.float32)
        seg_row = lax.dynamic_slice_in_dim(segment_ids, group, 1, 0)[0]
        member = (seg_row[:, None] == labels[None, :]).astype(jnp.float32)
        sums = jnp.einsum('te,ti,tj->eij', member, rows_out, rows_in).reshape(EX_DEV, R * R)
        counts = lax.optimization_barrier(jnp.sum(member, axis=0))
        return (sums / counts[:, None]).astype(jnp.bfloat16)
    query_logs = lax.map(one_group, jnp.arange(N_DP, dtype=jnp.int32)).reshape(EX_DEV * N_DP, R * R)
    doc_labels = jnp.arange(DOCS, dtype=jnp.int32)

    def score_block(block):
        rows = lax.dynamic_slice_in_dim(train_logs, block * N_DEV, N_DEV, 0)
        owners = lax.dynamic_slice_in_dim(doc_ids, block * N_DEV, N_DEV, 0)
        part_scores = jnp.dot(query_logs, rows.T, preferred_element_type=jnp.float32) * 0.125
        hot = (owners[:, None] == doc_labels[None, :]).astype(jnp.float32)
        return (part_scores, jnp.dot(part_scores, hot, precision=lax.Precision.HIGHEST))
    blocks, partial_docs = lax.map(score_block, jnp.arange(N_DP, dtype=jnp.int32))
    scores = jnp.transpose(blocks, (1, 0, 2)).reshape(EX_DEV * N_DP, N_DEV * N_DP)
    doc_influence = lax.optimization_barrier(jnp.sum(partial_docs, axis=0)) / math.sqrt(N_DEV * N_DP / DOCS)
    return (scores, doc_influence)
```

```python
import math

import jax
import jax.numpy as jnp
from jax import lax
from jax.sharding import Mesh
from jax.sharding import PartitionSpec as P

EX_DEV = 24
DOCS = 256
AXES = ("z", "yl", "yh", "x", "c")
SIZES = (16, 2, 2, 4, 2)
DP = ("z", "yl")
TENSOR = ("yh", "x", "c")
BF16 = jnp.bfloat16
F32 = jnp.float32


def swap(value, axis):
    return lax.ppermute(value, axis, [(0, 1), (1, 0)])


def exchange(value, axes):
    return lax.all_to_all(value, axes, 0, 0, tiled=True)


def split(value):
    high = lax.reduce_precision(value, 8, 7)
    return high.astype(BF16), (value - high).astype(BF16)


def dot_t(left, right):
    return lax.dot_general(left, right, (((1,), (1,)), ((), ())), preferred_element_type=F32)


def per_device(activations, out_grads, proj_in, proj_out, segment_ids, train_logs, doc_ids):
    yh, x, c = (lax.axis_index(name) for name in TENSOR)
    position = (yh * 4 + x) * 2 + c
    tokens = activations.shape[0]
    rank = proj_in.shape[1]
    logs, width = train_logs.shape

    blocks = train_logs.reshape(2, 4, 2, logs // 16, width)

    def rows_for(target):
        def block(row, col):
            return lax.dynamic_slice(blocks, (row, target, col, 0, 0), (1, 1, 1, logs // 16, width)).reshape(logs // 16, width)

        return jnp.concatenate([block(1 - yh, 1 - c), block(yh, 1 - c), block(1 - yh, c), block(yh, c)])

    rows = [rows_for(x)]
    for d in range(1, 4):
        rows.append(lax.ppermute(rows_for((x + d) % 4), "x", [(i, (i + d) % 4) for i in range(4)]))

    part = jnp.concatenate(
        [
            jnp.dot(activations, proj_in, preferred_element_type=F32),
            jnp.dot(out_grads, proj_out, preferred_element_type=F32),
        ],
        axis=1,
    )
    chunk = tokens // 16
    owners = jnp.pad(doc_ids.astype(F32).reshape(-1, 2 * rank), ((0, 6), (0, 0)))
    first = jnp.concatenate(
        [part.reshape(16, chunk, 2 * rank), jnp.broadcast_to(owners[None], (16, 8, 2 * rank))], axis=1
    )
    first = exchange(first.reshape(16 * (chunk + 8), 2 * rank), TENSOR).reshape(16, chunk + 8, 2 * rank)
    own = jnp.sum(first[:, :chunk], axis=0).astype(BF16)
    all_owners = first[:, chunk : chunk + 2].reshape(logs).astype(jnp.int32)
    both = exchange(jnp.broadcast_to(own[None], (16, chunk, 2 * rank)).reshape(tokens, 2 * rank), TENSOR)
    in_proj = both[:, :rank]
    out_proj = both[:, rank:]

    seg_row = segment_ids[0]
    labels = jnp.arange(EX_DEV, dtype=jnp.int32)
    hot = seg_row[:, None] == labels[None, :]
    counts = jnp.sum(hot.astype(F32), axis=0)
    block_rank = rank // 16
    own_out = lax.dynamic_slice_in_dim(out_proj, position * block_rank, block_rank, 1)
    masked = (hot.astype(BF16)[:, :, None] * own_out[:, None, :]).reshape(tokens, EX_DEV * block_rank)
    log_sums = jnp.einsum("ta,tj->aj", masked, in_proj, preferred_element_type=F32)
    query_block = (log_sums.reshape(EX_DEV, block_rank * rank) / counts[:, None]).astype(BF16)

    doc_hot = (jnp.arange(DOCS, dtype=jnp.int32)[:, None] == all_owners[None, :]).astype(BF16)
    doc_sums = jnp.dot(doc_hot, train_logs, preferred_element_type=F32)
    doc_high, doc_low = split(doc_sums)
    own_docs = DOCS // 32
    second = jnp.concatenate(
        [
            jnp.broadcast_to(query_block[None], (32, EX_DEV, width)),
            doc_high.reshape(32, own_docs, width),
            doc_low.reshape(32, own_docs, width),
        ],
        axis=1,
    )
    each = EX_DEV + 2 * own_docs
    second = exchange(second.reshape(32 * each, width), DP).reshape(32, each, width)
    queries = second[:, :EX_DEV].reshape(32 * EX_DEV, width)
    total_docs = jnp.sum(second[:, EX_DEV:].astype(F32), axis=0)
    total_docs = total_docs[:own_docs] + total_docs[own_docs:]
    high, low = split(total_docs)
    doc_part = dot_t(high, queries) + dot_t(low, queries)

    high, low = split(doc_part)
    tail = jnp.concatenate([high, low]).reshape(-1, width)
    height = queries.shape[0]
    third = jnp.concatenate([queries, tail])
    third = exchange(jnp.broadcast_to(third[None], (4, *third.shape)).reshape(-1, width), "x")
    third = third.reshape(4, -1, width)
    doc_part = jnp.sum(third[:, height:].reshape(4, 2 * own_docs, height).astype(F32), axis=0)
    doc_part = doc_part[:own_docs] + doc_part[own_docs:]
    doc_part = doc_part + swap(doc_part, "c")
    doc_part = doc_part + swap(doc_part, "yh")

    wide = jnp.concatenate([third[(x - d) % 4, :height] for d in range(4)], axis=1)
    stored = jnp.concatenate(rows, axis=1)
    half = stored.shape[0] // 2
    quarter = half // 2
    away = dot_t(wide, stored[:half]).astype(BF16)
    away = swap(away, "c")
    kept = dot_t(wide, stored[half:]) + away.astype(F32)
    far = swap(kept[:, :quarter].astype(BF16), "yh")
    scores = (kept[:, quarter:] + far.astype(F32)) * 0.125

    total_rows = logs * 32
    final = (doc_part * (0.125 / math.sqrt(total_rows / DOCS))).astype(BF16)
    final = exchange(jnp.broadcast_to(final[None], (32, own_docs, height)).reshape(DOCS, height), DP)
    doc_influence = final.T.astype(F32)
    return (scores, doc_influence)


def solution(mesh):
    inner = Mesh(mesh.devices.reshape(SIZES), AXES)
    placed = (
        P(DP, TENSOR),
        P(DP, TENSOR),
        P(TENSOR, None),
        P(TENSOR, None),
        P(DP, None),
        P(DP, TENSOR),
        P(AXES),
    )
    return jax.shard_map(
        per_device,
        mesh=inner,
        in_specs=placed,
        out_specs=(P(None, AXES), P()),
        check_vma=False,
    )
```

```python
import functools
import math

import jax
import jax.numpy as jnp
from jax import lax
from jax.experimental import pallas as pl
from jax.experimental.pallas import tpu as pltpu
from jax.sharding import Mesh
from jax.sharding import PartitionSpec as P

EX_DEV = 24
DOCS = 256
AXES = ("zh", "zl", "yl", "yh", "x", "c")
SIZES = (4, 4, 2, 2, 4, 2)
DP = ("zh", "zl", "yl")
NEAR = ("zl", "yl")
TENSOR = ("yh", "x", "c")
BF16 = jnp.bfloat16
F32 = jnp.float32


def swap(value, axis):
    return lax.ppermute(value, axis, [(0, 1), (1, 0)])


def exchange(value, axes):
    shape = value.shape
    flat = value.reshape(shape[0] * shape[1], shape[2])
    return lax.all_to_all(flat, axes, 0, 0, tiled=True).reshape(shape)


def to_all(value, members):
    return jnp.broadcast_to(value[None], (members, *value.shape))


def split(value):
    high = lax.reduce_precision(value, 8, 7)
    return high.astype(BF16), (value - high).astype(BF16)


def dot_t(left, right):
    return lax.dot_general(left, right, (((1,), (1,)), ((), ())), preferred_element_type=F32)


def partial_kernel(first, tile, place_ref, queries_ref, *refs):
    stored, out_ref = refs[:4], refs[4]
    height, count = out_ref.shape
    x = place_ref[0]
    for start in range(0, height, tile):
        total = None
        for d in range(4):
            left = queries_ref[lax.rem(x + 4 - d, 4), pl.ds(start, tile), :]
            term = dot_t(left, stored[d][pl.ds(first, count), :])
            total = term if total is None else total + term
        out_ref[pl.ds(start, tile), :] = total.astype(out_ref.dtype)


def partial(place, queries, stored, height, first, count, dtype):
    vmem = pl.BlockSpec(memory_space=pltpu.VMEM)
    return pl.pallas_call(
        functools.partial(partial_kernel, first, 128),
        out_shape=jax.ShapeDtypeStruct((height, count), dtype),
        in_specs=[pl.BlockSpec(memory_space=pltpu.SMEM)] + [vmem] * 5,
        out_specs=vmem,
        compiler_params=pltpu.CompilerParams(vmem_limit_bytes=32 * 1024 * 1024),
        cost_estimate=pl.CostEstimate(flops=2 * height * count * 1024, bytes_accessed=5 << 20, transcendentals=0),
    )(place, queries, *stored)


def per_device(activations, out_grads, proj_in, proj_out, segment_ids, train_logs, doc_ids):
    yh, x, c = (lax.axis_index(name) for name in TENSOR)
    position = (yh * 4 + x) * 2 + c
    tokens = activations.shape[0]
    rank = proj_in.shape[1]
    logs, width = train_logs.shape

    part = jnp.concatenate(
        [
            jnp.dot(activations, proj_in, preferred_element_type=F32),
            jnp.dot(out_grads, proj_out, preferred_element_type=F32),
        ],
        axis=1,
    )
    chunk = tokens // 16
    owners = jnp.pad(doc_ids.astype(F32).reshape(-1, 2 * rank), ((0, 6), (0, 0)))
    first = jnp.concatenate([part.reshape(16, chunk, 2 * rank), to_all(owners, 16)], axis=1)
    first = exchange(first, TENSOR)
    own = jnp.sum(first[:, :chunk], axis=0).astype(BF16)
    all_owners = first[:, chunk : chunk + 2].reshape(logs).astype(jnp.int32)
    both = exchange(to_all(own, 16), TENSOR).reshape(tokens, 2 * rank)
    in_proj = both[:, :rank]
    out_proj = both[:, rank:]

    seg_row = segment_ids[0]
    labels = jnp.arange(EX_DEV, dtype=jnp.int32)
    hot = seg_row[:, None] == labels[None, :]
    counts = jnp.sum(hot.astype(F32), axis=0)
    block_rank = rank // 16
    own_out = lax.dynamic_slice_in_dim(out_proj, position * block_rank, block_rank, 1)
    masked = (hot.astype(BF16)[:, :, None] * own_out[:, None, :]).reshape(tokens, EX_DEV * block_rank)
    log_sums = jnp.einsum("ta,tj->aj", masked, in_proj, preferred_element_type=F32)
    query_block = (log_sums.reshape(EX_DEV, block_rank * rank) / counts[:, None]).astype(BF16)

    doc_hot = (jnp.arange(DOCS, dtype=jnp.int32)[:, None] == all_owners[None, :]).astype(BF16)
    high, low = split(jnp.dot(doc_hot, train_logs, preferred_element_type=F32))
    far = jnp.concatenate(
        [to_all(query_block, 4), high.reshape(4, DOCS // 4, width), low.reshape(4, DOCS // 4, width)], axis=1
    )

    blocks = train_logs.reshape(2, 4, 2, logs // 16, width)

    def rows_for(target):
        def block(row, col):
            return lax.dynamic_slice(blocks, (row, target, col, 0, 0), (1, 1, 1, logs // 16, width)).reshape(logs // 16, width)

        return jnp.concatenate([block(1 - yh, 1 - c), block(yh, 1 - c), block(1 - yh, c), block(yh, c)])

    far, *moving = lax.optimization_barrier((far, *(rows_for((x + d) % 4) for d in range(1, 4))))
    far = exchange(far, "zh")
    stored = [rows_for(x)]
    for d in range(1, 4):
        stored.append(lax.ppermute(moving[d - 1], "x", [(i, (i + d) % 4) for i in range(4)]))

    docs = jnp.sum(far[:, EX_DEV:].astype(F32), axis=0)
    high, low = split(docs[: DOCS // 4] + docs[DOCS // 4 :])
    own_docs = DOCS // 32
    near = jnp.concatenate(
        [
            to_all(far[:, :EX_DEV].reshape(4 * EX_DEV, width), 8),
            high.reshape(8, own_docs, width),
            low.reshape(8, own_docs, width),
        ],
        axis=1,
    )
    near, stored[1], stored[3] = lax.optimization_barrier((near, stored[1], stored[3]))
    near = exchange(near, NEAR)
    queries = near[:, : 4 * EX_DEV].reshape(8, 4, EX_DEV, width).transpose(1, 0, 2, 3).reshape(32 * EX_DEV, width)
    docs = jnp.sum(near[:, 4 * EX_DEV :].astype(F32), axis=0)
    high, low = split(docs[:own_docs] + docs[own_docs:])
    doc_part = dot_t(high, queries) + dot_t(low, queries)

    height = queries.shape[0]
    high, low = split(doc_part)
    third = jnp.concatenate([queries, high.reshape(-1, width), low.reshape(-1, width)])
    third, *stored = lax.optimization_barrier((third, *stored))
    third = exchange(to_all(third, 4), "x")
    doc_part = jnp.sum(third[:, height:].astype(F32), axis=0).reshape(2, own_docs, height)
    doc_part = doc_part[0] + doc_part[1]
    doc_part = doc_part + swap(doc_part, "c")
    doc_part = doc_part + swap(doc_part, "yh")

    place = x.reshape(1)
    half = logs // 8
    away = swap(partial(place, third, stored, height, 0, half, BF16), "c")
    kept = partial(place, third, stored, height, half, half, F32) + away.astype(F32)
    quarter = half // 2
    beyond = swap(kept[:, :quarter].astype(BF16), "yh")
    scores = (kept[:, quarter:] + beyond.astype(F32)) * 0.125

    scale = 0.125 / math.sqrt(logs * 32 / DOCS)
    own_half = lax.dynamic_slice_in_dim(doc_part, c * (height // 2), height // 2, 1)
    final = exchange(to_all((own_half * scale).astype(BF16), 32), DP).reshape(DOCS, height // 2)
    final = lax.all_gather(final, "c", axis=0)
    doc_influence = final.transpose(0, 2, 1).reshape(height, DOCS).astype(F32)
    return (scores, doc_influence)


def solution(mesh):
    inner = Mesh(mesh.devices.reshape(SIZES), AXES)
    placed = (
        P(DP, TENSOR),
        P(DP, TENSOR),
        P(TENSOR, None),
        P(TENSOR, None),
        P(DP, None),
        P(DP, TENSOR),
        P(AXES),
    )
    return jax.shard_map(
        per_device,
        mesh=inner,
        in_specs=placed,
        out_specs=(P(None, AXES), P()),
        check_vma=False,
    )
```

```python
import functools
import math

import jax
import jax.numpy as jnp
from jax import lax
from jax.experimental import pallas as pl
from jax.experimental.pallas import tpu as pltpu
from jax.sharding import Mesh
from jax.sharding import PartitionSpec as P

EX_DEV = 24
DOCS = 256
AXES = ("zh", "zl", "yl", "yh", "x", "c")
SIZES = (4, 4, 2, 2, 4, 2)
DP = ("zh", "zl", "yl")
NEAR = ("zl", "yl")
TENSOR = ("yh", "x", "c")
BF16 = jnp.bfloat16
F32 = jnp.float32


def swap(value, axis):
    return lax.ppermute(value, axis, [(0, 1), (1, 0)])


def exchange(value, axes):
    shape = value.shape
    flat = value.reshape(shape[0] * shape[1], shape[2])
    return lax.all_to_all(flat, axes, 0, 0, tiled=True).reshape(shape)


def to_all(value, members):
    return jnp.broadcast_to(value[None], (members, *value.shape))


def split(value):
    high = lax.reduce_precision(value, 8, 7)
    return high.astype(BF16), (value - high).astype(BF16)


def dot_t(left, right):
    return lax.dot_general(left, right, (((1,), (1,)), ((), ())), preferred_element_type=F32)


def partial_kernel(tile, place_ref, queries_ref, *refs):
    stored, (away_ref, kept_ref) = refs[:4], refs[4:]
    height, half = away_ref.shape
    x = place_ref[0]
    for first, out_ref in ((0, away_ref), (half, kept_ref)):
        for start in range(0, height, tile):
            total = None
            for d in range(4):
                left = queries_ref[lax.rem(x + 4 - d, 4), pl.ds(start, tile), :]
                term = dot_t(left, stored[d][pl.ds(first, half), :])
                total = term if total is None else total + term
            out_ref[pl.ds(start, tile), :] = total.astype(out_ref.dtype)


def partial(place, queries, stored):
    height, half = queries.shape[1], stored[0].shape[0] // 2
    vmem = pl.BlockSpec(memory_space=pltpu.VMEM)
    return pl.pallas_call(
        functools.partial(partial_kernel, 128),
        out_shape=(jax.ShapeDtypeStruct((height, half), BF16), jax.ShapeDtypeStruct((height, half), F32)),
        in_specs=[pl.BlockSpec(memory_space=pltpu.SMEM)] + [vmem] * 5,
        out_specs=(vmem, vmem),
        compiler_params=pltpu.CompilerParams(vmem_limit_bytes=32 * 1024 * 1024),
        cost_estimate=pl.CostEstimate(flops=1024, bytes_accessed=1024, transcendentals=0),
    )(place, queries, *stored)


def per_device(activations, out_grads, proj_in, proj_out, segment_ids, train_logs, doc_ids):
    yh, x, c = (lax.axis_index(name) for name in TENSOR)
    position = (yh * 4 + x) * 2 + c
    tokens = activations.shape[0]
    rank = proj_in.shape[1]
    logs, width = train_logs.shape

    part = jnp.concatenate(
        [
            jnp.dot(activations, proj_in, preferred_element_type=F32),
            jnp.dot(out_grads, proj_out, preferred_element_type=F32),
        ],
        axis=1,
    )
    chunk = tokens // 16
    owners = jnp.pad(doc_ids.astype(F32).reshape(-1, 2 * rank), ((0, 6), (0, 0)))
    first = jnp.concatenate([part.reshape(16, chunk, 2 * rank), to_all(owners, 16)], axis=1)
    first = exchange(first, TENSOR)
    own = jnp.sum(first[:, :chunk], axis=0).astype(BF16)
    all_owners = first[:, chunk : chunk + 2].reshape(logs).astype(jnp.int32)
    both = exchange(to_all(own, 16), TENSOR).reshape(tokens, 2 * rank)
    in_proj = both[:, :rank]
    out_proj = both[:, rank:]

    seg_row = segment_ids[0]
    labels = jnp.arange(EX_DEV, dtype=jnp.int32)
    hot = seg_row[:, None] == labels[None, :]
    counts = jnp.sum(hot.astype(F32), axis=0)
    block_rank = rank // 16
    own_out = lax.dynamic_slice_in_dim(out_proj, position * block_rank, block_rank, 1)
    masked = (hot.astype(BF16)[:, :, None] * own_out[:, None, :]).reshape(tokens, EX_DEV * block_rank)
    log_sums = jnp.einsum("ta,tj->aj", masked, in_proj, preferred_element_type=F32)
    query_block = (log_sums.reshape(EX_DEV, block_rank * rank) / counts[:, None]).astype(BF16)

    doc_hot = (jnp.arange(DOCS, dtype=jnp.int32)[:, None] == all_owners[None, :]).astype(BF16)
    doc_sums = jnp.dot(doc_hot, train_logs, preferred_element_type=F32).astype(BF16)
    far = jnp.concatenate([to_all(query_block, 4), doc_sums.reshape(4, DOCS // 4, width)], axis=1)

    blocks = train_logs.reshape(2, 4, 2, logs // 16, width)

    def rows_for(target):
        def block(row, col):
            return lax.dynamic_slice(blocks, (row, target, col, 0, 0), (1, 1, 1, logs // 16, width)).reshape(logs // 16, width)

        return jnp.concatenate([block(1 - yh, 1 - c), block(yh, 1 - c), block(1 - yh, c), block(yh, c)])

    far, *moving = lax.optimization_barrier((far, *(rows_for((x + d) % 4) for d in range(1, 4))))
    far = exchange(far, "zh")
    stored = [rows_for(x)]
    for d in range(1, 4):
        stored.append(lax.ppermute(moving[d - 1], "x", [(i, (i + d) % 4) for i in range(4)]))

    docs = jnp.sum(far[:, EX_DEV:].astype(F32), axis=0)
    high, low = split(docs)
    own_docs = DOCS // 32
    near = jnp.concatenate(
        [
            to_all(far[:, :EX_DEV].reshape(4 * EX_DEV, width), 8),
            high.reshape(8, own_docs, width),
            low.reshape(8, own_docs, width),
        ],
        axis=1,
    )
    near, stored[2] = lax.optimization_barrier((near, stored[2]))
    near = exchange(near, NEAR)
    queries = near[:, : 4 * EX_DEV].reshape(8, 4, EX_DEV, width).transpose(1, 0, 2, 3).reshape(32 * EX_DEV, width)
    docs = jnp.sum(near[:, 4 * EX_DEV :].astype(F32), axis=0)
    high, low = split(docs[:own_docs] + docs[own_docs:])
    doc_part = dot_t(high, queries) + dot_t(low, queries)

    height = queries.shape[0]
    third, doc_part, stored[1], stored[3] = lax.optimization_barrier((queries, doc_part, stored[1], stored[3]))
    third = exchange(to_all(third, 4), "x")

    doc_part = doc_part.reshape(own_docs, 2, height // 2)
    doc_half = lax.dynamic_index_in_dim(doc_part, c, 1, keepdims=False) + swap(
        lax.dynamic_index_in_dim(doc_part, 1 - c, 1, keepdims=False), "c"
    )
    from_left = jnp.stack(
        [doc_half] + [lax.ppermute(doc_half, "x", [(i, (i + d) % 4) for i in range(4)]) for d in range(1, 4)]
    )
    parts = [lax.dynamic_index_in_dim(from_left, (x + 4 - i) % 4, 0, keepdims=False) for i in range(4)]
    doc_half = (parts[0] + parts[1]) + (parts[2] + parts[3])
    doc_half = doc_half + swap(doc_half, "yh")

    third, doc_half = lax.optimization_barrier((third, doc_half))
    away, kept = partial(x.reshape(1), third, stored)
    kept = kept + swap(away, "c").astype(F32)
    quarter = kept.shape[1] // 2
    beyond = swap(kept[:, :quarter].astype(BF16), "yh")
    scores = (kept[:, quarter:] + beyond.astype(F32)) * 0.125

    scale = 0.125 / math.sqrt(logs * 32 / DOCS)
    final = exchange(to_all((doc_half * scale).astype(BF16), 32), DP).reshape(DOCS, height // 2)
    final, scores = lax.optimization_barrier((final, scores))
    final = lax.all_gather(final, "c", axis=0)
    doc_influence = final.transpose(0, 2, 1).reshape(height, DOCS).astype(F32)
    return (scores, doc_influence)


def solution(mesh):
    inner = Mesh(mesh.devices.reshape(SIZES), AXES)
    placed = (
        P(DP, TENSOR),
        P(DP, TENSOR),
        P(TENSOR, None),
        P(TENSOR, None),
        P(DP, None),
        P(DP, TENSOR),
        P(AXES),
    )
    return jax.shard_map(
        per_device,
        mesh=inner,
        in_specs=placed,
        out_specs=(P(None, AXES), P()),
        check_vma=False,
    )
```

```python
import math

import jax
import jax.numpy as jnp
from jax import lax
from jax.experimental import pallas as pl
from jax.sharding import Mesh
from jax.sharding import PartitionSpec as P

EX_DEV = 24
DOCS = 256
AXES = ("zh", "zl", "yl", "yh", "x", "c")
SIZES = (4, 4, 2, 2, 4, 2)
DP = ("zh", "zl", "yl")
NEAR = ("zl", "yl")
TENSOR = ("yh", "x", "c")
BF16 = jnp.bfloat16
F32 = jnp.float32


def swap(value, axis):
    return lax.ppermute(value, axis, [(0, 1), (1, 0)])


def along_x(value, distance):
    return lax.ppermute(value, "x", [(i, (i + distance) % 4) for i in range(4)]) if distance else value


def exchange(value, axes):
    shape = value.shape
    flat = value.reshape(shape[0] * shape[1], shape[2])
    return lax.all_to_all(flat, axes, 0, 0, tiled=True).reshape(shape)


def to_all(value, members):
    return jnp.broadcast_to(value[None], (members, *value.shape))


def split(value):
    high = lax.reduce_precision(value, 8, 7)
    return high.astype(BF16), (value - high).astype(BF16)


def dot_t(left, right):
    return lax.dot_general(left, right, (((1,), (1,)), ((), ())), preferred_element_type=F32)


def partial_kernel(own, left, upper, lower, right, *refs):
    stored, (away_ref, kept_ref) = refs[:4], refs[4:]
    half = away_ref.shape[1]
    first_half = pl.program_id(0) < pl.num_programs(0) // 2
    across = jnp.where(first_half, upper[...], lower[...])
    queries = (own[...], left[...], across, right[...])
    for first, out_ref in ((0, away_ref), (half, kept_ref)):
        terms = [dot_t(q, t[pl.ds(first, half), :]) for q, t in zip(queries, stored)]
        out_ref[...] = ((terms[0] + terms[1]) + (terms[2] + terms[3])).astype(out_ref.dtype)


def partial(queries, stored):
    (height, width), count = queries[0].shape, stored[0].shape[0]
    tile, half = 128, count // 2
    steps = height // tile
    rows = pl.BlockSpec((tile, width), lambda i: (i, 0))
    upper = pl.BlockSpec((tile, width), lambda i: (jnp.minimum(i, steps // 2 - 1), 0))
    lower = pl.BlockSpec((tile, width), lambda i: (jnp.maximum(i - steps // 2, 0), 0))
    whole = pl.BlockSpec((count, width), lambda i: (0, 0))
    out = pl.BlockSpec((tile, half), lambda i: (i, 0))
    return pl.pallas_call(
        partial_kernel,
        grid=(steps,),
        out_shape=(jax.ShapeDtypeStruct((height, half), BF16), jax.ShapeDtypeStruct((height, half), F32)),
        in_specs=[rows, rows, upper, lower, rows] + [whole] * 4,
        out_specs=(out, out),
        cost_estimate=pl.CostEstimate(flops=8 * height * count * width, bytes_accessed=6 << 20, transcendentals=0),
    )(*queries, *stored)


def per_device(activations, out_grads, proj_in, proj_out, segment_ids, train_logs, doc_ids):
    yh, x, c = (lax.axis_index(name) for name in TENSOR)
    position = (yh * 4 + x) * 2 + c
    tokens = activations.shape[0]
    rank = proj_in.shape[1]
    logs, width = train_logs.shape

    part = jnp.concatenate(
        [
            jnp.dot(activations, proj_in, preferred_element_type=F32),
            jnp.dot(out_grads, proj_out, preferred_element_type=F32),
        ],
        axis=1,
    )
    chunk = tokens // 16
    owners = jnp.pad(doc_ids.astype(F32).reshape(-1, 2 * rank), ((0, 6), (0, 0)))
    first = jnp.concatenate([part.reshape(16, chunk, 2 * rank), to_all(owners, 16)], axis=1)
    first = exchange(first, TENSOR)
    own = jnp.sum(first[:, :chunk], axis=0).astype(BF16)
    all_owners = first[:, chunk : chunk + 2].reshape(logs).astype(jnp.int32)
    both = exchange(to_all(own, 16), TENSOR).reshape(tokens, 2 * rank)
    in_proj = both[:, :rank]
    out_proj = both[:, rank:]

    seg_row = segment_ids[0]
    labels = jnp.arange(EX_DEV, dtype=jnp.int32)
    hot = seg_row[:, None] == labels[None, :]
    counts = jnp.sum(hot.astype(F32), axis=0)
    block_rank = rank // 16
    own_out = lax.dynamic_slice_in_dim(out_proj, position * block_rank, block_rank, 1)
    masked = (hot.astype(BF16)[:, :, None] * own_out[:, None, :]).reshape(tokens, EX_DEV * block_rank)
    log_sums = jnp.einsum("ta,tj->aj", masked, in_proj, preferred_element_type=F32)
    query_block = (log_sums.reshape(EX_DEV, block_rank * rank) / counts[:, None]).astype(BF16)

    doc_hot = (jnp.arange(DOCS, dtype=jnp.int32)[:, None] == all_owners[None, :]).astype(BF16)
    doc_sums = jnp.dot(doc_hot, train_logs, preferred_element_type=F32).astype(BF16)
    far = jnp.concatenate([to_all(query_block, 4), doc_sums.reshape(4, DOCS // 4, width)], axis=1)

    blocks = train_logs.reshape(2, 4, 2, logs // 16, width)

    def rows_for(target):
        def block(row, col):
            return lax.dynamic_slice(blocks, (row, target, col, 0, 0), (1, 1, 1, logs // 16, width)).reshape(logs // 16, width)

        return jnp.concatenate([block(1 - yh, 1 - c), block(yh, 1 - c), block(1 - yh, c), block(yh, c)])

    stored = [along_x(rows_for((x + d) % 4), d) for d in range(4)]
    far, stored[1], stored[3] = lax.optimization_barrier((far, stored[1], stored[3]))
    far = exchange(far, "zh")

    docs = jnp.sum(far[:, EX_DEV:].astype(F32), axis=0)
    high, low = split(docs)
    own_docs = DOCS // 32
    near = jnp.concatenate(
        [
            to_all(far[:, :EX_DEV].reshape(4 * EX_DEV, width), 8),
            high.reshape(8, own_docs, width),
            low.reshape(8, own_docs, width),
        ],
        axis=1,
    )
    near, stored[2] = lax.optimization_barrier((near, stored[2]))
    near = exchange(near, NEAR)
    queries = near[:, : 4 * EX_DEV].reshape(8, 4, EX_DEV, width).transpose(1, 0, 2, 3).reshape(32 * EX_DEV, width)
    docs = jnp.sum(near[:, 4 * EX_DEV :].astype(F32), axis=0)
    high, low = split(docs[:own_docs] + docs[own_docs:])
    doc_part = dot_t(high, queries) + dot_t(low, queries)

    height = queries.shape[0]
    share = height // 16
    left, right = along_x(queries, 1), along_x(queries, 3)
    doc_part = jnp.pad(doc_part.reshape(own_docs, 16, share), ((0, 0), (0, 0), (0, 128 - share))).transpose(1, 0, 2)
    doc_part = jnp.sum(exchange(doc_part, TENSOR), axis=0)
    scale = 0.125 / math.sqrt(logs * 32 / DOCS)
    doc_part = to_all((doc_part * scale).astype(BF16), 32)
    doc_part, left, right = lax.optimization_barrier((doc_part, left, right))
    influence = exchange(doc_part, DP).reshape(DOCS, 128)[:, :share].T
    across = [along_x(left[: height // 2], 1), along_x(right[height // 2 :], 3)]
    *across, influence = lax.optimization_barrier((*across, influence))

    away, kept = partial([queries, left, *across, right], stored)
    kept = kept + swap(away, "c").astype(F32)
    quarter = kept.shape[1] // 2
    beyond = swap(kept[:, :quarter].astype(BF16), "yh")
    scores = (kept[:, quarter:] + beyond.astype(F32)) * 0.125
    doc_influence = exchange(to_all(influence, 16), TENSOR).reshape(height, DOCS).astype(F32)
    return (scores, doc_influence)


def solution(mesh):
    inner = Mesh(mesh.devices.reshape(SIZES), AXES)
    placed = (
        P(DP, TENSOR),
        P(DP, TENSOR),
        P(TENSOR, None),
        P(TENSOR, None),
        P(DP, None),
        P(DP, TENSOR),
        P(AXES),
    )
    return jax.shard_map(
        per_device,
        mesh=inner,
        in_specs=placed,
        out_specs=(P(None, AXES), P()),
        check_vma=False,
    )
```

```python
import math

import jax
import jax.numpy as jnp
from jax import lax
from jax.experimental import pallas as pl
from jax.sharding import Mesh
from jax.sharding import PartitionSpec as P

EX_DEV = 24
DOCS = 256
AXES = ("z", "yl", "yh", "x", "c")
SIZES = (16, 2, 2, 4, 2)
DP = ("z", "yl")
TENSOR = ("yh", "x", "c")
BF16 = jnp.bfloat16
F32 = jnp.float32


def swap(value, axis):
    return lax.ppermute(value, axis, [(0, 1), (1, 0)])


def along_x(value, distance):
    return lax.ppermute(value, "x", [(i, (i + distance) % 4) for i in range(4)]) if distance else value


def exchange(value, axes):
    shape = value.shape
    flat = value.reshape(shape[0] * shape[1], shape[2])
    return lax.all_to_all(flat, axes, 0, 0, tiled=True).reshape(shape)


def to_all(value, members):
    return jnp.broadcast_to(value[None], (members, *value.shape))


def split(value):
    high = lax.reduce_precision(value, 8, 7)
    return high.astype(BF16), (value - high).astype(BF16)


def dot_t(left, right):
    return lax.dot_general(left, right, (((1,), (1,)), ((), ())), preferred_element_type=F32)


def partial_kernel(own, left, upper, lower, right, *refs):
    stored, (away_ref, kept_ref) = refs[:4], refs[4:]
    half = away_ref.shape[1]
    first_half = pl.program_id(0) < pl.num_programs(0) // 2
    across = jnp.where(first_half, upper[...], lower[...])
    queries = (own[...], left[...], across, right[...])
    for first, out_ref in ((0, away_ref), (half, kept_ref)):
        terms = [dot_t(q, t[pl.ds(first, half), :]) for q, t in zip(queries, stored)]
        out_ref[...] = ((terms[0] + terms[1]) + (terms[2] + terms[3])).astype(out_ref.dtype)


def partial(queries, stored):
    (height, width), count = queries[0].shape, stored[0].shape[0]
    tile, half = height // 2, count // 2
    steps = height // tile
    rows = pl.BlockSpec((tile, width), lambda i: (i, 0))
    upper = pl.BlockSpec((tile, width), lambda i: (jnp.minimum(i, steps // 2 - 1), 0))
    lower = pl.BlockSpec((tile, width), lambda i: (jnp.maximum(i - steps // 2, 0), 0))
    whole = pl.BlockSpec((count, width), lambda i: (0, 0))
    out = pl.BlockSpec((tile, half), lambda i: (i, 0))
    return pl.pallas_call(
        partial_kernel,
        grid=(steps,),
        out_shape=(jax.ShapeDtypeStruct((height, half), BF16), jax.ShapeDtypeStruct((height, half), F32)),
        in_specs=[rows, rows, upper, lower, rows] + [whole] * 4,
        out_specs=(out, out),
        cost_estimate=pl.CostEstimate(flops=8 * height * count * width, bytes_accessed=6 << 20, transcendentals=0),
    )(*queries, *stored)


def per_device(activations, out_grads, proj_in, proj_out, segment_ids, train_logs, doc_ids):
    yh, x, c = (lax.axis_index(name) for name in TENSOR)
    position = (yh * 4 + x) * 2 + c
    tokens = activations.shape[0]
    rank = proj_in.shape[1]
    logs, width = train_logs.shape

    part = jnp.concatenate(
        [
            jnp.dot(activations, proj_in, preferred_element_type=F32),
            jnp.dot(out_grads, proj_out, preferred_element_type=F32),
        ],
        axis=1,
    )
    chunk = tokens // 16
    owners = jnp.pad(doc_ids.astype(F32).reshape(-1, 2 * rank), ((0, 6), (0, 0)))
    first = jnp.concatenate([part.reshape(16, chunk, 2 * rank), to_all(owners, 16)], axis=1)
    first = exchange(first, TENSOR)
    own = jnp.sum(first[:, :chunk], axis=0).astype(BF16)
    all_owners = first[:, chunk : chunk + 2].reshape(logs).astype(jnp.int32)
    both = exchange(to_all(own, 16), TENSOR).reshape(tokens, 2 * rank)
    in_proj = both[:, :rank]
    out_proj = both[:, rank:]

    seg_row = segment_ids[0]
    labels = jnp.arange(EX_DEV, dtype=jnp.int32)
    hot = seg_row[:, None] == labels[None, :]
    counts = jnp.sum(hot.astype(F32), axis=0)
    block_rank = rank // 16
    own_out = lax.dynamic_slice_in_dim(out_proj, position * block_rank, block_rank, 1)
    masked = (hot.astype(BF16)[:, :, None] * own_out[:, None, :]).reshape(tokens, EX_DEV * block_rank)
    log_sums = jnp.einsum("ta,tj->aj", masked, in_proj, preferred_element_type=F32)
    query_block = (log_sums.reshape(EX_DEV, block_rank * rank) / counts[:, None]).astype(BF16)

    doc_hot = (jnp.arange(DOCS, dtype=jnp.int32)[:, None] == all_owners[None, :]).astype(BF16)
    doc_sums = jnp.dot(doc_hot, train_logs, preferred_element_type=F32).astype(BF16)
    own_docs = DOCS // 32
    second = jnp.concatenate([to_all(query_block, 32), doc_sums.reshape(32, own_docs, width)], axis=1)

    blocks = train_logs.reshape(2, 4, 2, logs // 16, width)

    def rows_for(target):
        def block(row, col):
            return lax.dynamic_slice(blocks, (row, target, col, 0, 0), (1, 1, 1, logs // 16, width)).reshape(logs // 16, width)

        return jnp.concatenate([block(1 - yh, 1 - c), block(yh, 1 - c), block(1 - yh, c), block(yh, c)])

    stored = [along_x(rows_for((x + d) % 4), d) for d in range(4)]
    second, stored[1], stored[3] = lax.optimization_barrier((second, stored[1], stored[3]))
    second = exchange(second, DP)
    second, stored[2] = lax.optimization_barrier((second, stored[2]))
    queries = second[:, :EX_DEV].reshape(32 * EX_DEV, width)
    height = queries.shape[0]

    left, right = along_x(queries, 1), along_x(queries, 3)

    high, low = split(jnp.sum(second[:, EX_DEV:].astype(F32), axis=0))
    doc_part = dot_t(high, queries) + dot_t(low, queries)
    doc_part = jnp.sum(exchange(to_all(doc_part, 16), TENSOR), axis=0)
    doc_part = (doc_part * (0.125 / math.sqrt(logs * 32 / DOCS))).astype(BF16)
    doc_part, left, right = lax.optimization_barrier((doc_part, left, right))
    doc_influence = exchange(to_all(doc_part, 32), DP).reshape(DOCS, height).T.astype(F32)

    across = [along_x(left[: height // 2], 1), along_x(right[height // 2 :], 3)]

    away, kept = partial([queries, left, *across, right], stored)
    kept = kept + swap(away, "c").astype(F32)
    quarter = kept.shape[1] // 2
    beyond = swap(kept[:, :quarter].astype(BF16), "yh")
    scores = (kept[:, quarter:] + beyond.astype(F32)) * 0.125
    return (scores, doc_influence)


def solution(mesh):
    inner = Mesh(mesh.devices.reshape(SIZES), AXES)
    placed = (
        P(DP, TENSOR),
        P(DP, TENSOR),
        P(TENSOR, None),
        P(TENSOR, None),
        P(DP, None),
        P(DP, TENSOR),
        P(AXES),
    )
    return jax.shard_map(
        per_device,
        mesh=inner,
        in_specs=placed,
        out_specs=(P(None, AXES), P()),
        check_vma=False,
    )
```

```python
import math

import jax
import jax.numpy as jnp
from jax import lax
from jax.experimental import pallas as pl
from jax.sharding import Mesh
from jax.sharding import PartitionSpec as P

EX_DEV = 24
DOCS = 256
AXES = ("z", "yl", "yh", "x", "c")
SIZES = (16, 2, 2, 4, 2)
DP = ("z", "yl")
TENSOR = ("yh", "x", "c")
BF16 = jnp.bfloat16
F32 = jnp.float32


def swap(value, axis):
    return lax.ppermute(value, axis, [(0, 1), (1, 0)])


def along_x(value, distance):
    return lax.ppermute(value, "x", [(i, (i + distance) % 4) for i in range(4)]) if distance else value


def exchange(value, axes):
    shape = value.shape
    flat = value.reshape(shape[0] * shape[1], shape[2])
    return lax.all_to_all(flat, axes, 0, 0, tiled=True).reshape(shape)


def to_all(value, members):
    return jnp.broadcast_to(value[None], (members, *value.shape))


def split(value):
    high = lax.reduce_precision(value, 8, 7)
    return high.astype(BF16), (value - high).astype(BF16)


def dot_t(left, right):
    return lax.dot_general(left, right, (((1,), (1,)), ((), ())), preferred_element_type=F32)


def partial_kernel(own, left, upper, lower, right, *refs):
    stored, (away_ref, kept_ref) = refs[:4], refs[4:]
    half = away_ref.shape[1]
    first_half = pl.program_id(0) < pl.num_programs(0) // 2
    across = jnp.where(first_half, upper[...], lower[...])
    queries = (own[...], left[...], across, right[...])
    for first, out_ref in ((0, away_ref), (half, kept_ref)):
        terms = [dot_t(q, t[pl.ds(first, half), :]) for q, t in zip(queries, stored)]
        out_ref[...] = ((terms[0] + terms[1]) + (terms[2] + terms[3])).astype(out_ref.dtype)


def partial(queries, stored):
    (height, width), count = queries[0].shape, stored[0].shape[0]
    tile, half = height // 2, count // 2
    steps = height // tile
    rows = pl.BlockSpec((tile, width), lambda i: (i, 0))
    upper = pl.BlockSpec((tile, width), lambda i: (jnp.minimum(i, steps // 2 - 1), 0))
    lower = pl.BlockSpec((tile, width), lambda i: (jnp.maximum(i - steps // 2, 0), 0))
    whole = pl.BlockSpec((count, width), lambda i: (0, 0))
    out = pl.BlockSpec((tile, half), lambda i: (i, 0))
    return pl.pallas_call(
        partial_kernel,
        grid=(steps,),
        out_shape=(jax.ShapeDtypeStruct((height, half), BF16), jax.ShapeDtypeStruct((height, half), F32)),
        in_specs=[rows, rows, upper, lower, rows] + [whole] * 4,
        out_specs=(out, out),
        cost_estimate=pl.CostEstimate(flops=8 * height * count * width, bytes_accessed=6 << 20, transcendentals=0),
    )(*queries, *stored)


def per_device(activations, out_grads, proj_in, proj_out, segment_ids, train_logs, doc_ids):
    yh, x, c = (lax.axis_index(name) for name in TENSOR)
    position = (yh * 4 + x) * 2 + c
    tokens = activations.shape[0]
    rank = proj_in.shape[1]
    logs, width = train_logs.shape

    part = jnp.concatenate(
        [
            jnp.dot(activations, proj_in, preferred_element_type=F32),
            jnp.dot(out_grads, proj_out, preferred_element_type=F32),
        ],
        axis=1,
    )
    chunk = tokens // 16
    owners = jnp.pad(doc_ids.astype(F32).reshape(-1, 2 * rank), ((0, 6), (0, 0)))
    first = jnp.concatenate([part.reshape(16, chunk, 2 * rank), to_all(owners, 16)], axis=1)
    first = exchange(first, TENSOR)
    own = jnp.sum(first[:, :chunk], axis=0).astype(BF16)
    all_owners = first[:, chunk : chunk + 2].reshape(logs).astype(jnp.int32)
    both = exchange(to_all(own, 16), TENSOR).reshape(tokens, 2 * rank)
    in_proj = both[:, :rank]
    out_proj = both[:, rank:]

    seg_row = segment_ids[0]
    labels = jnp.arange(EX_DEV, dtype=jnp.int32)
    hot = seg_row[:, None] == labels[None, :]
    counts = jnp.sum(hot.astype(F32), axis=0)
    block_rank = rank // 16
    own_out = lax.dynamic_slice_in_dim(out_proj, position * block_rank, block_rank, 1)
    masked = (hot.astype(BF16)[:, :, None] * own_out[:, None, :]).reshape(tokens, EX_DEV * block_rank)
    log_sums = jnp.einsum("ta,tj->aj", masked, in_proj, preferred_element_type=F32)
    query_block = (log_sums.reshape(EX_DEV, block_rank * rank) / counts[:, None]).astype(BF16)

    doc_hot = (jnp.arange(DOCS, dtype=jnp.int32)[:, None] == all_owners[None, :]).astype(BF16)
    doc_sums = jnp.dot(doc_hot, train_logs, preferred_element_type=F32).astype(BF16)
    own_docs = DOCS // 32
    second = jnp.concatenate([to_all(query_block, 32), doc_sums.reshape(32, own_docs, width)], axis=1)

    blocks = train_logs.reshape(2, 4, 2, logs // 16, width)

    def rows_for(target):
        def block(row, col):
            return lax.dynamic_slice(blocks, (row, target, col, 0, 0), (1, 1, 1, logs // 16, width)).reshape(logs // 16, width)

        return jnp.concatenate([block(1 - yh, 1 - c), block(yh, 1 - c), block(1 - yh, c), block(yh, c)])

    stored = [along_x(rows_for((x + d) % 4), d) for d in range(4)]
    second, stored[1], stored[3] = lax.optimization_barrier((second, stored[1], stored[3]))
    second = exchange(second, DP)
    second, stored[2] = lax.optimization_barrier((second, stored[2]))
    queries = second[:, :EX_DEV].reshape(32 * EX_DEV, width)
    height = queries.shape[0]

    left, right = along_x(queries, 1), along_x(queries, 3)

    high, low = split(jnp.sum(second[:, EX_DEV:].astype(F32), axis=0))
    doc_part = dot_t(high, queries) + dot_t(low, queries)
    halves = doc_part.reshape(own_docs, 2, height // 2).transpose(1, 0, 2)
    halves = jnp.broadcast_to(halves[None], (8, *halves.shape)).reshape(16, own_docs, height // 2)
    halves = jnp.sum(exchange(halves, TENSOR), axis=0)
    halves = (halves * (0.125 / math.sqrt(logs * 32 / DOCS))).astype(BF16)
    halves, left, right = lax.optimization_barrier((halves, left, right))
    halves = exchange(to_all(halves, 32), DP).reshape(DOCS, height // 2)

    across = [along_x(left[: height // 2], 1), along_x(right[height // 2 :], 3)]

    *across, halves = lax.optimization_barrier((*across, halves))
    away, kept = partial([queries, left, *across, right], stored)
    kept = kept + swap(away, "c").astype(F32)
    quarter = kept.shape[1] // 2
    beyond = swap(kept[:, :quarter].astype(BF16), "yh")
    doc_influence = lax.all_gather(halves, "c", axis=0).transpose(0, 2, 1).reshape(height, DOCS).astype(F32)
    scores = (kept[:, quarter:] + beyond.astype(F32)) * 0.125
    return (scores, doc_influence)


def solution(mesh):
    inner = Mesh(mesh.devices.reshape(SIZES), AXES)
    placed = (
        P(DP, TENSOR),
        P(DP, TENSOR),
        P(TENSOR, None),
        P(TENSOR, None),
        P(DP, None),
        P(DP, TENSOR),
        P(AXES),
    )
    return jax.shard_map(
        per_device,
        mesh=inner,
        in_specs=placed,
        out_specs=(P(None, AXES), P()),
        check_vma=False,
    )
```

```python
import math

import jax
import jax.numpy as jnp
from jax import lax
from jax.experimental import pallas as pl
from jax.sharding import Mesh
from jax.sharding import PartitionSpec as P

EX_DEV = 24
DOCS = 256
AXES = ("z", "yl", "yh", "x", "c")
SIZES = (16, 2, 2, 4, 2)
DP = ("z", "yl")
TENSOR = ("yh", "x", "c")
BF16 = jnp.bfloat16
F32 = jnp.float32


def swap(value, axis):
    return lax.ppermute(value, axis, [(0, 1), (1, 0)])


def along_x(value, distance):
    return lax.ppermute(value, "x", [(i, (i + distance) % 4) for i in range(4)]) if distance else value


def exchange(value, axes):
    shape = value.shape
    flat = value.reshape(shape[0] * shape[1], shape[2])
    return lax.all_to_all(flat, axes, 0, 0, tiled=True).reshape(shape)


def to_all(value, members):
    return jnp.broadcast_to(value[None], (members, *value.shape))


def split(value):
    high = lax.reduce_precision(value, 8, 7)
    return high.astype(BF16), (value - high).astype(BF16)


def dot_t(left, right):
    return lax.dot_general(left, right, (((1,), (1,)), ((), ())), preferred_element_type=F32)


def partial_kernel(own, left, upper, lower, right, *refs):
    stored, (away_ref, kept_ref) = refs[:4], refs[4:]
    half = away_ref.shape[1]
    first_half = pl.program_id(0) < pl.num_programs(0) // 2
    across = jnp.where(first_half, upper[...], lower[...])
    queries = (own[...], left[...], across, right[...])
    for first, out_ref in ((0, away_ref), (half, kept_ref)):
        terms = [dot_t(q, t[pl.ds(first, half), :]) for q, t in zip(queries, stored)]
        out_ref[...] = ((terms[0] + terms[1]) + (terms[2] + terms[3])).astype(out_ref.dtype)


def partial(queries, stored):
    (height, width), count = queries[0].shape, stored[0].shape[0]
    tile, half = height // 2, count // 2
    steps = height // tile
    rows = pl.BlockSpec((tile, width), lambda i: (i, 0))
    upper = pl.BlockSpec((tile, width), lambda i: (jnp.minimum(i, steps // 2 - 1), 0))
    lower = pl.BlockSpec((tile, width), lambda i: (jnp.maximum(i - steps // 2, 0), 0))
    whole = pl.BlockSpec((count, width), lambda i: (0, 0))
    out = pl.BlockSpec((tile, half), lambda i: (i, 0))
    return pl.pallas_call(
        partial_kernel,
        grid=(steps,),
        out_shape=(jax.ShapeDtypeStruct((height, half), BF16), jax.ShapeDtypeStruct((height, half), F32)),
        in_specs=[rows, rows, upper, lower, rows] + [whole] * 4,
        out_specs=(out, out),
        cost_estimate=pl.CostEstimate(flops=8 * height * count * width, bytes_accessed=6 << 20, transcendentals=0),
    )(*queries, *stored)


def per_device(activations, out_grads, proj_in, proj_out, segment_ids, train_logs, doc_ids):
    yh, x, c = (lax.axis_index(name) for name in TENSOR)
    position = (yh * 4 + x) * 2 + c
    tokens = activations.shape[0]
    rank = proj_in.shape[1]
    logs, width = train_logs.shape

    part = jnp.concatenate(
        [
            jnp.dot(activations, proj_in, preferred_element_type=F32),
            jnp.dot(out_grads, proj_out, preferred_element_type=F32),
        ],
        axis=1,
    )
    chunk = tokens // 16
    owners = jnp.pad(doc_ids.astype(F32).reshape(-1, 2 * rank), ((0, 6), (0, 0)))
    first = jnp.concatenate([part.reshape(16, chunk, 2 * rank), to_all(owners, 16)], axis=1)
    first = exchange(first, TENSOR)
    own = jnp.sum(first[:, :chunk], axis=0).astype(BF16)
    all_owners = first[:, chunk : chunk + 2].reshape(logs).astype(jnp.int32)
    both = exchange(to_all(own, 16), TENSOR).reshape(tokens, 2 * rank)
    in_proj = both[:, :rank]
    out_proj = both[:, rank:]

    seg_row = segment_ids[0]
    labels = jnp.arange(EX_DEV, dtype=jnp.int32)
    hot = seg_row[:, None] == labels[None, :]
    counts = jnp.sum(hot.astype(F32), axis=0)
    block_rank = rank // 16
    own_out = lax.dynamic_slice_in_dim(out_proj, position * block_rank, block_rank, 1)
    masked = (hot.astype(BF16)[:, :, None] * own_out[:, None, :]).reshape(tokens, EX_DEV * block_rank)
    log_sums = jnp.einsum("ta,tj->aj", masked, in_proj, preferred_element_type=F32)
    query_block = (log_sums.reshape(EX_DEV, block_rank * rank) / counts[:, None]).astype(BF16)

    doc_hot = (jnp.arange(DOCS, dtype=jnp.int32)[:, None] == all_owners[None, :]).astype(BF16)
    doc_sums = jnp.dot(doc_hot, train_logs, preferred_element_type=F32).astype(BF16)
    own_docs = DOCS // 32
    second = jnp.concatenate([to_all(query_block, 32), doc_sums.reshape(32, own_docs, width)], axis=1)

    blocks = train_logs.reshape(2, 4, 2, logs // 16, width)

    def rows_for(target):
        def block(row, col):
            return lax.dynamic_slice(blocks, (row, target, col, 0, 0), (1, 1, 1, logs // 16, width)).reshape(logs // 16, width)

        return jnp.concatenate([block(1 - yh, 1 - c), block(yh, 1 - c), block(1 - yh, c), block(yh, c)])

    stored = [along_x(rows_for((x + d) % 4), d) for d in range(4)]
    second, stored[1], stored[3] = lax.optimization_barrier((second, stored[1], stored[3]))
    second = exchange(second, DP)
    second, stored[2] = lax.optimization_barrier((second, stored[2]))
    queries = second[:, :EX_DEV].reshape(32 * EX_DEV, width)
    height = queries.shape[0]

    left, right = along_x(queries, 1), along_x(queries, 3)

    high, low = split(jnp.sum(second[:, EX_DEV:].astype(F32), axis=0))
    doc_part = dot_t(high, queries) + dot_t(low, queries)
    halves = doc_part.reshape(own_docs, 2, height // 2).transpose(1, 0, 2)
    halves = jnp.broadcast_to(halves[None], (8, *halves.shape)).reshape(16, own_docs, height // 2)
    halves = jnp.sum(exchange(halves, TENSOR), axis=0)
    halves = (halves * (0.125 / math.sqrt(logs * 32 / DOCS))).astype(BF16)
    halves, left, right = lax.optimization_barrier((halves, left, right))
    halves = exchange(to_all(halves, 32), DP).reshape(DOCS, height // 2)

    across = [along_x(left[: height // 2], 1), along_x(right[height // 2 :], 3)]

    away, kept = partial([queries, left, *across, right], stored)
    away, halves = lax.optimization_barrier((away, halves))
    away = swap(away, "c")
    quarter = kept.shape[1] // 2
    beyond = swap((kept[:, :quarter] + away[:, :quarter].astype(F32)).astype(BF16), "yh")
    doc_influence = lax.all_gather(halves, "c", axis=0).transpose(0, 2, 1).reshape(height, DOCS).astype(F32)
    scores = (kept[:, quarter:] + away[:, quarter:].astype(F32) + beyond.astype(F32)) * 0.125
    return (scores, doc_influence)


def solution(mesh):
    inner = Mesh(mesh.devices.reshape(SIZES), AXES)
    placed = (
        P(DP, TENSOR),
        P(DP, TENSOR),
        P(TENSOR, None),
        P(TENSOR, None),
        P(DP, None),
        P(DP, TENSOR),
        P(AXES),
    )
    return jax.shard_map(
        per_device,
        mesh=inner,
        in_specs=placed,
        out_specs=(P(None, AXES), P()),
        check_vma=False,
    )
```

```python
import math

import jax
import jax.numpy as jnp
from jax import lax
from jax.experimental import pallas as pl
from jax.sharding import Mesh
from jax.sharding import PartitionSpec as P

EX_DEV = 24
DOCS = 256
AXES = ("z", "yl", "yh", "x", "c")
SIZES = (16, 2, 2, 4, 2)
DP = ("z", "yl")
TENSOR = ("yh", "x", "c")
BF16 = jnp.bfloat16
F32 = jnp.float32


def swap(value, axis):
    return lax.ppermute(value, axis, [(0, 1), (1, 0)])


def along_x(value, distance):
    return lax.ppermute(value, "x", [(i, (i + distance) % 4) for i in range(4)]) if distance else value


def exchange(value, axes):
    shape = value.shape
    flat = value.reshape(shape[0] * shape[1], shape[2])
    return lax.all_to_all(flat, axes, 0, 0, tiled=True).reshape(shape)


def to_all(value, members):
    return jnp.broadcast_to(value[None], (members, *value.shape))


def split(value):
    high = lax.reduce_precision(value, 8, 7)
    return high.astype(BF16), (value - high).astype(BF16)


def dot_t(left, right):
    return lax.dot_general(left, right, (((1,), (1,)), ((), ())), preferred_element_type=F32)


def partial_kernel(own, left, upper, lower, right, *refs):
    stored, (away_ref, kept_ref) = refs[:4], refs[4:]
    half = away_ref.shape[1]
    first_half = pl.program_id(0) < pl.num_programs(0) // 2
    across = jnp.where(first_half, upper[...], lower[...])
    queries = (own[...], left[...], across, right[...])
    for first, out_ref in ((0, away_ref), (half, kept_ref)):
        terms = [dot_t(q, t[pl.ds(first, half), :]) for q, t in zip(queries, stored)]
        out_ref[...] = ((terms[0] + terms[1]) + (terms[2] + terms[3])).astype(out_ref.dtype)


def partial(queries, stored):
    (height, width), count = queries[0].shape, stored[0].shape[0]
    tile, half = height // 2, count // 2
    steps = height // tile
    rows = pl.BlockSpec((tile, width), lambda i: (i, 0))
    upper = pl.BlockSpec((tile, width), lambda i: (jnp.minimum(i, steps // 2 - 1), 0))
    lower = pl.BlockSpec((tile, width), lambda i: (jnp.maximum(i - steps // 2, 0), 0))
    whole = pl.BlockSpec((count, width), lambda i: (0, 0))
    out = pl.BlockSpec((tile, half), lambda i: (i, 0))
    return pl.pallas_call(
        partial_kernel,
        grid=(steps,),
        out_shape=(jax.ShapeDtypeStruct((height, half), BF16), jax.ShapeDtypeStruct((height, half), F32)),
        in_specs=[rows, rows, upper, lower, rows] + [whole] * 4,
        out_specs=(out, out),
        cost_estimate=pl.CostEstimate(flops=8 * height * count * width, bytes_accessed=6 << 20, transcendentals=0),
    )(*queries, *stored)


def per_device(activations, out_grads, proj_in, proj_out, segment_ids, train_logs, doc_ids):
    yh, x, c = (lax.axis_index(name) for name in TENSOR)
    position = (yh * 4 + x) * 2 + c
    tokens = activations.shape[0]
    rank = proj_in.shape[1]
    logs, width = train_logs.shape

    part = jnp.concatenate(
        [
            jnp.dot(activations, proj_in, preferred_element_type=F32),
            jnp.dot(out_grads, proj_out, preferred_element_type=F32),
        ],
        axis=1,
    )
    chunk = tokens // 16
    owners = jnp.pad(doc_ids.astype(F32).reshape(-1, 2 * rank), ((0, 6), (0, 0)))
    first = jnp.concatenate([part.reshape(16, chunk, 2 * rank), to_all(owners, 16)], axis=1)
    first = exchange(first, TENSOR)
    own = jnp.sum(first[:, :chunk], axis=0).astype(BF16)
    all_owners = first[:, chunk : chunk + 2].reshape(logs).astype(jnp.int32)
    both = exchange(to_all(own, 16), TENSOR).reshape(tokens, 2 * rank)
    in_proj = both[:, :rank]
    out_proj = both[:, rank:]

    seg_row = segment_ids[0]
    labels = jnp.arange(EX_DEV, dtype=jnp.int32)
    hot = seg_row[:, None] == labels[None, :]
    counts = jnp.sum(hot.astype(F32), axis=0)
    block_rank = rank // 16
    own_out = lax.dynamic_slice_in_dim(out_proj, position * block_rank, block_rank, 1)
    masked = (hot.astype(BF16)[:, :, None] * own_out[:, None, :]).reshape(tokens, EX_DEV * block_rank)
    log_sums = jnp.einsum("ta,tj->aj", masked, in_proj, preferred_element_type=F32)
    query_block = (log_sums.reshape(EX_DEV, block_rank * rank) / counts[:, None]).astype(BF16)

    doc_hot = (jnp.arange(DOCS, dtype=jnp.int32)[:, None] == all_owners[None, :]).astype(BF16)
    doc_sums = jnp.dot(doc_hot, train_logs, preferred_element_type=F32).astype(BF16)
    own_docs = DOCS // 32
    second = jnp.concatenate([to_all(query_block, 32), doc_sums.reshape(32, own_docs, width)], axis=1)

    blocks = train_logs.reshape(2, 4, 2, logs // 16, width)

    def rows_for(target):
        def block(row, col):
            return lax.dynamic_slice(blocks, (row, target, col, 0, 0), (1, 1, 1, logs // 16, width)).reshape(logs // 16, width)

        return jnp.concatenate([block(1 - yh, 1 - c), block(yh, 1 - c), block(1 - yh, c), block(yh, c)])

    stored = [along_x(rows_for((x + d) % 4), d) for d in range(4)]
    second, stored[1] = lax.optimization_barrier((second, stored[1]))
    second = exchange(second, DP)
    second, stored[2], stored[3] = lax.optimization_barrier((second, stored[2], stored[3]))
    queries = second[:, :EX_DEV].reshape(32 * EX_DEV, width)
    height = queries.shape[0]

    left, right = along_x(queries, 1), along_x(queries, 3)

    high, low = split(jnp.sum(second[:, EX_DEV:].astype(F32), axis=0))
    doc_part = dot_t(high, queries) + dot_t(low, queries)
    share = height // 8
    halves = jnp.pad(doc_part.reshape(own_docs, 8, share), ((0, 0), (0, 0), (0, 128 - share))).transpose(1, 0, 2)
    halves = jnp.broadcast_to(halves[None], (2, *halves.shape)).reshape(16, own_docs, 128)
    halves = jnp.sum(exchange(halves, TENSOR), axis=0)
    halves = (halves * (0.125 / math.sqrt(logs * 32 / DOCS))).astype(BF16)
    halves, left, right = lax.optimization_barrier((halves, left, right))
    halves = exchange(to_all(halves, 32), DP).reshape(DOCS, 128)[:, :share].T

    across = [along_x(left[: height // 2], 1), along_x(right[height // 2 :], 3)]

    away, kept = partial([queries, left, *across, right], stored)
    away, halves = lax.optimization_barrier((away, halves))
    away = swap(away, "c")
    quarter = kept.shape[1] // 2
    beyond = swap((kept[:, :quarter] + away[:, :quarter].astype(F32)).astype(BF16), "yh")
    doc_influence = exchange(to_all(halves, 8), ("x", "c")).reshape(height, DOCS).astype(F32)
    scores = (kept[:, quarter:] + away[:, quarter:].astype(F32) + beyond.astype(F32)) * 0.125
    return (scores, doc_influence)


def solution(mesh):
    inner = Mesh(mesh.devices.reshape(SIZES), AXES)
    placed = (
        P(DP, TENSOR),
        P(DP, TENSOR),
        P(TENSOR, None),
        P(TENSOR, None),
        P(DP, None),
        P(DP, TENSOR),
        P(AXES),
    )
    return jax.shard_map(
        per_device,
        mesh=inner,
        in_specs=placed,
        out_specs=(P(None, AXES), P()),
        check_vma=False,
    )
```

```python
import math

import jax
import jax.numpy as jnp
from jax import lax
from jax.experimental import pallas as pl
from jax.sharding import Mesh
from jax.sharding import PartitionSpec as P

EX_DEV = 24
DOCS = 256
AXES = ("z", "yl", "yh", "x", "c")
SIZES = (16, 2, 2, 4, 2)
DP = ("z", "yl")
TENSOR = ("yh", "x", "c")
BF16 = jnp.bfloat16
F32 = jnp.float32


def swap(value, axis):
    return lax.ppermute(value, axis, [(0, 1), (1, 0)])


def along_x(value, distance):
    return lax.ppermute(value, "x", [(i, (i + distance) % 4) for i in range(4)]) if distance else value


def exchange(value, axes):
    shape = value.shape
    flat = value.reshape(shape[0] * shape[1], shape[2])
    return lax.all_to_all(flat, axes, 0, 0, tiled=True).reshape(shape)


def to_all(value, members):
    return jnp.broadcast_to(value[None], (members, *value.shape))


def split(value):
    high = lax.reduce_precision(value, 8, 7)
    return high.astype(BF16), (value - high).astype(BF16)


def dot_t(left, right):
    return lax.dot_general(left, right, (((1,), (1,)), ((), ())), preferred_element_type=F32)


def partial_kernel(own, left, upper, lower, right, *refs):
    stored, outs = refs[:4], refs[4:]
    first_half = pl.program_id(0) < pl.num_programs(0) // 2
    across = jnp.where(first_half, upper[...], lower[...])
    queries = (own[...], left[...], across, right[...])
    first = 0
    for out_ref in outs:
        count = out_ref.shape[1]
        terms = [dot_t(q, t[pl.ds(first, count), :]) for q, t in zip(queries, stored)]
        out_ref[...] = ((terms[0] + terms[1]) + (terms[2] + terms[3])).astype(out_ref.dtype)
        first += count


def partial(queries, stored):
    (height, width), count = queries[0].shape, stored[0].shape[0]
    tile, half = height // 2, count // 2
    steps = height // tile
    rows = pl.BlockSpec((tile, width), lambda i: (i, 0))
    upper = pl.BlockSpec((tile, width), lambda i: (jnp.minimum(i, steps // 2 - 1), 0))
    lower = pl.BlockSpec((tile, width), lambda i: (jnp.maximum(i - steps // 2, 0), 0))
    whole = pl.BlockSpec((count, width), lambda i: (0, 0))
    outs = ((half, BF16), (half // 2, F32), (half // 2, F32))
    return pl.pallas_call(
        partial_kernel,
        grid=(steps,),
        out_shape=tuple(jax.ShapeDtypeStruct((height, n), kind) for n, kind in outs),
        in_specs=[rows, rows, upper, lower, rows] + [whole] * 4,
        out_specs=tuple(pl.BlockSpec((tile, n), lambda i: (i, 0)) for n, _ in outs),
        cost_estimate=pl.CostEstimate(flops=8 * height * count * width, bytes_accessed=6 << 20, transcendentals=0),
    )(*queries, *stored)


def per_device(activations, out_grads, proj_in, proj_out, segment_ids, train_logs, doc_ids):
    yh, x, c = (lax.axis_index(name) for name in TENSOR)
    position = (yh * 4 + x) * 2 + c
    tokens = activations.shape[0]
    rank = proj_in.shape[1]
    logs, width = train_logs.shape

    part = jnp.concatenate(
        [
            jnp.dot(activations, proj_in, preferred_element_type=F32),
            jnp.dot(out_grads, proj_out, preferred_element_type=F32),
        ],
        axis=1,
    )
    chunk = tokens // 16
    owners = jnp.pad(doc_ids.astype(F32).reshape(-1, 2 * rank), ((0, 6), (0, 0)))
    first = jnp.concatenate([part.reshape(16, chunk, 2 * rank), to_all(owners, 16)], axis=1)
    first = exchange(first, TENSOR)
    own = jnp.sum(first[:, :chunk], axis=0).astype(BF16)
    all_owners = first[:, chunk : chunk + 2].reshape(logs).astype(jnp.int32)
    both = exchange(to_all(own, 16), TENSOR).reshape(tokens, 2 * rank)
    in_proj = both[:, :rank]
    out_proj = both[:, rank:]

    seg_row = segment_ids[0]
    labels = jnp.arange(EX_DEV, dtype=jnp.int32)
    hot = seg_row[:, None] == labels[None, :]
    counts = jnp.sum(hot.astype(F32), axis=0)
    block_rank = rank // 16
    own_out = lax.dynamic_slice_in_dim(out_proj, position * block_rank, block_rank, 1)
    masked = (hot.astype(BF16)[:, :, None] * own_out[:, None, :]).reshape(tokens, EX_DEV * block_rank)
    log_sums = jnp.einsum("ta,tj->aj", masked, in_proj, preferred_element_type=F32)
    query_block = (log_sums.reshape(EX_DEV, block_rank * rank) / counts[:, None]).astype(BF16)

    doc_hot = (jnp.arange(DOCS, dtype=jnp.int32)[:, None] == all_owners[None, :]).astype(BF16)
    doc_sums = jnp.dot(doc_hot, train_logs, preferred_element_type=F32).astype(BF16)
    own_docs = DOCS // 32
    second = jnp.concatenate([to_all(query_block, 32), doc_sums.reshape(32, own_docs, width)], axis=1)

    blocks = train_logs.reshape(2, 4, 2, logs // 16, width)

    def rows_for(target):
        def block(row, col):
            return lax.dynamic_slice(blocks, (row, target, col, 0, 0), (1, 1, 1, logs // 16, width)).reshape(logs // 16, width)

        return jnp.concatenate([block(1 - yh, 1 - c), block(yh, 1 - c), block(1 - yh, c), block(yh, c)])

    stored = [along_x(rows_for((x + d) % 4), d) for d in range(4)]
    second, stored[1] = lax.optimization_barrier((second, stored[1]))
    second = exchange(second, DP)
    second, stored[2], stored[3] = lax.optimization_barrier((second, stored[2], stored[3]))
    queries = second[:, :EX_DEV].reshape(32 * EX_DEV, width)
    height = queries.shape[0]

    left, right = along_x(queries, 1), along_x(queries, 3)

    high, low = split(jnp.sum(second[:, EX_DEV:].astype(F32), axis=0))
    doc_part = dot_t(high, queries) + dot_t(low, queries)
    halves = doc_part.reshape(own_docs, 2, height // 2).transpose(1, 0, 2)
    halves = jnp.broadcast_to(halves[None], (8, *halves.shape)).reshape(16, own_docs, height // 2)
    halves = jnp.sum(exchange(halves, TENSOR), axis=0)
    halves = (halves * (0.125 / math.sqrt(logs * 32 / DOCS))).astype(BF16)
    halves, left, right = lax.optimization_barrier((halves, left, right))
    halves = exchange(to_all(halves, 32), DP).reshape(DOCS, height // 2)

    across = [along_x(left[: height // 2], 1), along_x(right[height // 2 :], 3)]

    away, far, near = partial([queries, left, *across, right], stored)
    away, halves = lax.optimization_barrier((away, halves))
    away = swap(away, "c")
    quarter = far.shape[1]
    beyond = swap((far + away[:, :quarter].astype(F32)).astype(BF16), "yh")
    doc_influence = lax.all_gather(halves, "c", axis=0).transpose(0, 2, 1).reshape(height, DOCS).astype(F32)
    scores = (near + away[:, quarter:].astype(F32) + beyond.astype(F32)) * 0.125
    return (scores, doc_influence)


def solution(mesh):
    inner = Mesh(mesh.devices.reshape(SIZES), AXES)
    placed = (
        P(DP, TENSOR),
        P(DP, TENSOR),
        P(TENSOR, None),
        P(TENSOR, None),
        P(DP, None),
        P(DP, TENSOR),
        P(AXES),
    )
    return jax.shard_map(
        per_device,
        mesh=inner,
        in_specs=placed,
        out_specs=(P(None, AXES), P()),
        check_vma=False,
    )
```
